32 devices in a mesh: fsdp: 16 (over z, y, x), tp: 2 (over core).
Axes of the slice: x: 2, y: 2, z: 4, core: 2. Of those that a mesh axis runs over, the one named last changes fastest.
Arguments:
- tokens: bfloat16 [4096, 2048], P(('fsdp', 'tp')), may hold values from -6 to 6
- norm_gain: float32 [2048], replicated, may hold values from 0.5 to 1.5
- in_weight: bfloat16 [2048, 6144], P(None, ('fsdp', 'tp')), may hold values from -0.125 to 0.125
- filter_taps: float32 [128, 128], P('tp'), may hold values from -0.5 to 0.5
- skip_gain: float32 [2048], P('tp'), may hold values from 0.5 to 2
Outputs:
- gated: bfloat16 [4096, 2048], P('fsdp', 'tp')
The draws below stay inside these ranges and needn't reach their ends.
All inputs are finite; a program needn't handle non-finite values.
Results may differ from the reference program's by a relative error of at most 0.007.
Values may be sent and summed in bfloat16 or wider, within the bound.
No kernel may reach another device: no remote copies, remote signals or barrier semaphores. Data moves between devices by JAX's collectives and lax.ppermute only.
A program may use at most 64 MiB of HBM per device.

```python
import math
import jax
import jax.numpy as jnp
from jax import lax

DIN = 2048
C = 2048
GROUP = 16
TAPS = 128
TOKENS = 4096
GROUPS = 128
N_FSDP = 16
N_TP = 2


def level_of(key, extent, pieces, least, top_value):
    factor_of = 1.0
    for axis_at, shards_of in pieces:
        heights = jax.random.uniform(jax.random.fold_in(jax.random.fold_in(key, 6), axis_at), (shards_of,), jnp.float32, least / len(pieces), top_value / len(pieces))
        factor_of = factor_of * jnp.repeat(jnp.exp(heights), extent[axis_at] // shards_of).reshape((-1,) + (1,) * (len(extent) - 1 - axis_at))
    return factor_of


def normal_values(rng, dims, width, most, cuts=(), kind=jnp.bfloat16):
    values = width * jax.random.normal(rng, dims, jnp.float32)
    if cuts:
        values = values * level_of(rng, dims, cuts, -0.22, 0.18)
    return jnp.clip(values, -most, most).astype(kind)


def setup_inputs(seed: int = 0) -> dict:
    seeds = jax.random.split(jax.random.key(seed), 6)
    return {
        "tokens": normal_values(seeds[0], (TOKENS, DIN), 1.0, 6.0, ((0, 32),)),
        "norm_gain": jnp.clip(1.0 + 0.1 * jax.random.normal(seeds[1], (DIN,), jnp.float32), 0.5, 1.5),
        "in_weight": normal_values(seeds[2], (DIN, 3 * C), DIN ** -0.5, 0.125, ((1, 32),)),
        "filter_taps": normal_values(seeds[3], (GROUPS, TAPS), TAPS ** -0.5, 0.5, ((0, 2),), jnp.float32),
        "skip_gain": jnp.clip(jnp.exp(math.log(2.0) - 1.3862944 * jax.random.uniform(seeds[4], (C,), jnp.float32) ** level_of(seeds[4], (C,), ((0, 2),), -0.2, 0.2)), 0.5, 2.0),
    }


def causal_blocks(extended, filter_taps):
    tap_count = filter_taps.shape[1]
    row_count = extended.shape[0] - tap_count
    channels = extended.shape[1]
    groups = filter_taps.shape[0]
    group_width = channels // groups
    offset = jnp.arange(tap_count)[:, None] - jnp.arange(tap_count)[None, :]
    near_taps = jnp.where(offset >= 0, filter_taps[:, jnp.clip(offset, 0, tap_count - 1)], 0.0)
    far_taps = jnp.where(offset < 0, filter_taps[:, jnp.clip(offset + tap_count, 0, tap_count - 1)], 0.0)
    widened = extended.astype(jnp.float32)
    block_shape = (row_count // tap_count, tap_count, groups, group_width)
    current = widened[tap_count:].reshape(block_shape)
    earlier = widened[:-tap_count].reshape(block_shape)
    result = jnp.einsum('gij,bjgc->bigc', near_taps, current, precision=lax.Precision.HIGHEST)
    result = result + jnp.einsum('gij,bjgc->bigc', far_taps, earlier, precision=lax.Precision.HIGHEST)
    return result.reshape(row_count, channels)

def reference(tokens, norm_gain, in_weight, filter_taps, skip_gain):
    features = tokens.astype(jnp.float32)
    power = lax.optimization_barrier(jnp.mean(features * features, axis=1, keepdims=True))
    normed = (features * lax.rsqrt(power + 1e-06) * norm_gain).astype(jnp.bfloat16)
    per_group = C // N_TP
    block_cols = 3 * C // (N_FSDP * N_TP)
    arranged = in_weight.reshape(DIN, N_FSDP, N_TP, block_cols).transpose(0, 2, 1, 3)
    arranged = arranged.reshape(DIN, N_TP, 3, per_group).transpose(2, 0, 1, 3).reshape(3, DIN, C)
    slice_width = 128
    slices = C // slice_width
    stacked = arranged.reshape(3, DIN, slices, slice_width).transpose(2, 0, 1, 3)
    slice_taps_all = filter_taps.reshape(slices, slice_width // GROUP, TAPS)
    slice_skips_all = skip_gain.reshape(slices, slice_width)

    def one_slice(operands):
        slice_weights, slice_taps, slice_skip = operands
        query = jnp.dot(normed, slice_weights[0], preferred_element_type=jnp.float32)
        keys = jnp.dot(normed, slice_weights[1], preferred_element_type=jnp.float32)
        values = jnp.dot(normed, slice_weights[2], preferred_element_type=jnp.float32)
        mixed = (keys * values).astype(jnp.bfloat16)
        padded = jnp.concatenate([jnp.zeros((TAPS, slice_width), mixed.dtype), mixed], axis=0)
        conv = causal_blocks(padded, slice_taps)
        return (query * (conv + slice_skip * mixed.astype(jnp.float32))).astype(jnp.bfloat16)
    results = lax.map(one_slice, (stacked, slice_taps_all, slice_skips_all))
    return results.transpose(1, 0, 2).reshape(TOKENS, C)
```

```python
import jax
import jax.numpy as jnp
from jax import lax
from jax.experimental import pallas as pl
from jax.experimental.pallas import tpu as pltpu
from jax.sharding import PartitionSpec as P

AXES = ("fsdp", "tp")
SIDE = 2
PLANE = SIDE * SIDE
STREAMS = 3
VMEM = pl.BlockSpec(memory_space=pltpu.VMEM)
SMEM = pl.BlockSpec(memory_space=pltpu.SMEM)


def passed_along(block, axis, distance):
    devices = range(lax.axis_size(axis))
    route = [(i - distance, i) for i in devices if i - distance in devices]
    return lax.ppermute(block, axis, route)


def causal_blocks(extended, filter_taps):
    tap_count = filter_taps.shape[1]
    row_count = extended.shape[0] - tap_count
    channels = extended.shape[1]
    groups = filter_taps.shape[0]
    group_width = channels // groups
    offset = jnp.arange(tap_count)[:, None] - jnp.arange(tap_count)[None, :]
    near_taps = jnp.where(offset >= 0, filter_taps[:, jnp.clip(offset, 0, tap_count - 1)], 0.0)
    far_taps = jnp.where(
        offset < 0, filter_taps[:, jnp.clip(offset + tap_count, 0, tap_count - 1)], 0.0
    )
    widened = extended.astype(jnp.float32)
    block_shape = (row_count // tap_count, tap_count, groups, group_width)
    current = widened[tap_count:].reshape(block_shape)
    earlier = widened[:-tap_count].reshape(block_shape)
    result = jnp.einsum("gij,bjgc->bigc", near_taps, current, precision=lax.Precision.HIGHEST)
    result = result + jnp.einsum(
        "gij,bjgc->bigc", far_taps, earlier, precision=lax.Precision.HIGHEST
    )
    return result.reshape(row_count, channels)


def normalized(tokens, norm_gain):
    features = tokens.astype(jnp.float32)
    power = jnp.mean(features * features, axis=1, keepdims=True)
    return (features * lax.rsqrt(power + 1e-06) * norm_gain).astype(jnp.bfloat16)


def general_shards(tokens, norm_gain, in_weight, filter_taps, skip_gain):
    tap_count = filter_taps.shape[1]
    normed = normalized(tokens, norm_gain)
    slab_rows = lax.all_gather(normed, "tp", axis=0, tiled=True)
    token_edge = passed_along(slab_rows[-tap_count:], "fsdp", 1)
    all_rows = jnp.concatenate([token_edge, slab_rows], axis=0)
    full_weight = lax.all_gather(in_weight, "fsdp", axis=1, tiled=True)
    proj_all = jnp.dot(all_rows, full_weight, preferred_element_type=jnp.float32)
    channels = proj_all.shape[1] // STREAMS
    edge_proj = proj_all[:tap_count]
    proj = proj_all[tap_count:]
    mixed_edge = (edge_proj[:, channels : 2 * channels] * edge_proj[:, 2 * channels :]).astype(
        jnp.bfloat16
    )
    mixed = (proj[:, channels : 2 * channels] * proj[:, 2 * channels :]).astype(jnp.bfloat16)
    query = proj[:, :channels]
    extended = jnp.concatenate([mixed_edge, mixed], axis=0)
    conv = causal_blocks(extended, filter_taps)
    return (query * (conv + skip_gain * mixed.astype(jnp.float32))).astype(jnp.bfloat16)


def moved(block, route):
    planes = lax.axis_size("fsdp") // PLANE
    cores = lax.axis_size("tp")

    def index(p, y, x, t):
        return ((p * SIDE + y) * SIDE + x) * cores + t

    pairs = []
    for p in range(planes):
        for y in range(SIDE):
            for x in range(SIDE):
                for t in range(cores):
                    target = route(p, y, x, t)
                    if target is not None and 0 <= target[0] < planes:
                        pairs.append((index(p, y, x, t), index(*target)))
    return lax.ppermute(block, AXES, pairs)


def to_x(p, y, x, t):
    return p, y, 1 - x, t


def to_y(p, y, x, t):
    return p, 1 - y, x, t


def to_xy(p, y, x, t):
    return p, 1 - y, 1 - x, t


def to_core(p, y, x, t):
    return p, y, x, 1 - t


def to_pair(p, y, x, t):
    return p ^ 1, y, x, t


def to_middle(p, y, x, t):
    return (3 - p, y, x, t) if p in (1, 2) else None


def to_end(p, y, x, t):
    return ({1: 0, 2: 3}[p], y, x, t) if p in (1, 2) else None


def project(place, chunks, rows, held):
    chunk_cols, depth = chunks[0][0].shape
    blocks, block_rows = rows.shape[0] // 128, 128
    planes = lax.axis_size("fsdp") // PLANE
    piece = len(chunks) * chunk_cols
    flat = [c for options in chunks for c in options]

    def kernel(*refs):
        place_ref = refs[0]
        chunk_refs = refs[1 : 1 + len(flat)]
        rows_ref = refs[1 + len(flat)]
        out_ref = refs[-2]
        weights = refs[-1]
        at = 0
        for which, options in enumerate(chunks):
            value = chunk_refs[at][...]
            if len(options) == 2:
                value = jnp.where(place_ref[4] == 1, value, chunk_refs[at + 1][...])
            at += len(options)
            start = pl.multiple_of(place_ref[1 + which] * chunk_cols, chunk_cols)
            weights[pl.ds(start, chunk_cols), :] = value
        weight = weights[...]
        for first in range(0, blocks, 2):
            count = min(2, blocks - first)
            some = rows_ref[first * block_rows : (first + count) * block_rows, :]
            result = lax.dot_general(
                weight, some, (((1,), (1,)), ((), ())), preferred_element_type=jnp.float32
            )
            for k in range(count):
                out_ref[0, first + k] = result[:, k * block_rows : (k + 1) * block_rows]

    shape = (planes, blocks, piece, block_rows)
    operands = [*flat, rows]
    in_specs = [pl.BlockSpec(c.shape, lambda i, place: (0, 0)) for c in operands]
    aliases = {}
    if held is not None:
        aliases = {1 + len(operands): 0}
        operands.append(held)
        in_specs.append(pl.BlockSpec(memory_space=pl.ANY))
    return pl.pallas_call(
        kernel,
        out_shape=jax.ShapeDtypeStruct(shape, jnp.float32),
        grid_spec=pltpu.PrefetchScalarGridSpec(
            num_scalar_prefetch=1,
            grid=(1,),
            in_specs=in_specs,
            out_specs=pl.BlockSpec((1, *shape[1:]), lambda i, place: (place[0], 0, 0, 0)),
            scratch_shapes=[pltpu.VMEM((piece, depth), jnp.bfloat16)],
        ),
        input_output_aliases=aliases,
        cost_estimate=pl.CostEstimate(
            flops=2 * piece * depth * rows.shape[0],
            bytes_accessed=2 * rows.size + 4 * piece * rows.shape[0],
            transcendentals=0,
        ),
        name="project",
    )(place, *operands)


def filter_matrices(where, filter_taps, chunk_groups):
    tap_count = filter_taps.shape[1]
    groups = filter_taps.shape[0] // PLANE
    sections = groups // chunk_groups

    def kernel(where_ref, taps_ref, out_ref):
        member = where_ref[0]
        for section in range(sections):
            for k in range(chunk_groups):
                row = (section * PLANE + member) * chunk_groups + k
                taps = taps_ref[pl.ds(row, 1), :]
                padded = jnp.concatenate([taps, jnp.zeros_like(taps)], axis=1)
                wide = jnp.broadcast_to(padded, (2 * tap_count, 2 * tap_count))
                rolled = pltpu.roll(wide, tap_count, 1, stride=1, stride_axis=0)[:, :tap_count]
                high = rolled.astype(jnp.bfloat16)
                low = (rolled - high.astype(jnp.float32)).astype(jnp.bfloat16)
                g = section * chunk_groups + k
                out_ref[g, :, :tap_count] = high
                out_ref[g, :, tap_count:] = low

    return pl.pallas_call(
        kernel,
        out_shape=jax.ShapeDtypeStruct((groups, 2 * tap_count, 2 * tap_count), jnp.bfloat16),
        in_specs=[SMEM, VMEM],
        out_specs=VMEM,
        cost_estimate=pl.CostEstimate(
            flops=groups * 8 * tap_count * tap_count,
            bytes_accessed=groups * 8 * tap_count * tap_count,
            transcendentals=0,
        ),
        name="filters",
    )(where, filter_taps)


def mixed_and_gated(where, proj, matrices, skip, chunk_cols):
    planes, blocks, piece, taps = proj.shape
    sections = planes
    halo = blocks - 1
    slab_blocks = halo // PLANE
    width = matrices.shape[0]
    channels = sections * chunk_cols
    group = channels // width

    def kernel(where_ref, proj_ref, matrix_ref, skip_ref, *rest):
        outs, mixed_ref, left = rest[:PLANE], rest[PLANE], rest[PLANE + 1]
        member, core = where_ref[0], where_ref[1]

        def part(stream, section):
            b = stream * sections + section
            return b // STREAMS, (b % STREAMS) * chunk_cols

        for section in range(sections):
            kp, kr = part(1, section)
            vp, vr = part(2, section)
            for m in range(blocks):
                key = proj_ref[kp, m, kr : kr + chunk_cols, :]
                value = proj_ref[vp, m, vr : vr + chunk_cols, :]
                mixed_ref[m, section * chunk_cols : (section + 1) * chunk_cols, :] = (
                    key * value
                ).astype(jnp.bfloat16)
        currents, befores = [], []
        for r in range(halo):
            jj, h = r // slab_blocks, r % slab_blocks
            slab = jj ^ member
            currents.append(jj * slab_blocks + (h ^ core))
            if h > 0:
                befores.append(jj * slab_blocks + ((h - 1) ^ core))
            else:
                before = ((slab - 1) ^ member) * slab_blocks + ((slab_blocks - 1) ^ core)
                befores.append(jnp.where(slab == 0, halo, before))
        for g in range(width):
            lanes = slice(g * group, (g + 1) * group)
            for r in range(halo):
                left[g % 2, r * group : (r + 1) * group, :taps] = mixed_ref[befores[r], lanes, :]
                left[g % 2, r * group : (r + 1) * group, taps:] = mixed_ref[currents[r], lanes, :]
            both = jnp.dot(left[g % 2], matrix_ref[g], preferred_element_type=jnp.float32)
            conv = both[:, :taps] + both[:, taps:]
            section, inside = (g * group) // chunk_cols, (g * group) % chunk_cols
            qp, qr = part(0, section)
            gain = skip_ref[lanes, :]
            for r in range(halo):
                jj, h = r // slab_blocks, r % slab_blocks
                mixed = left[g % 2, r * group : (r + 1) * group, taps:].astype(jnp.float32)
                query = proj_ref[qp, currents[r], qr + inside : qr + inside + group, :]
                outs[jj][lanes, h * taps : (h + 1) * taps] = (
                    query * (conv[r * group : (r + 1) * group] + gain * mixed)
                ).astype(jnp.bfloat16)

    return pl.pallas_call(
        kernel,
        out_shape=[jax.ShapeDtypeStruct((channels, slab_blocks * taps), jnp.bfloat16)] * PLANE,
        in_specs=[SMEM, VMEM, VMEM, VMEM],
        out_specs=[VMEM] * PLANE,
        scratch_shapes=[
            pltpu.VMEM((blocks, channels, taps), jnp.bfloat16),
            pltpu.VMEM((2, halo * group, 2 * taps), jnp.bfloat16),
        ],
        name="gate",
    )(where, proj, matrices, skip)


def assembled(where, parts, chunk_cols):
    channels, rows = parts[0].shape
    sections = channels // chunk_cols

    def kernel(where_ref, *rest):
        sources, out_ref, ordered = rest[:PLANE], rest[PLANE], rest[PLANE + 1]
        for jj in range(PLANE):
            ordered[jj ^ where_ref[0]] = sources[jj][...].astype(jnp.float32)
        for section in range(sections):
            for pair in range(0, PLANE, 2):
                chunk = slice(section * chunk_cols, (section + 1) * chunk_cols)
                tall = jnp.concatenate([ordered[pair, chunk, :], ordered[pair + 1, chunk, :]], axis=0)
                at = (section * PLANE + pair) * chunk_cols
                out_ref[:, at : at + 2 * chunk_cols] = tall.T.astype(jnp.bfloat16)

    return pl.pallas_call(
        kernel,
        out_shape=jax.ShapeDtypeStruct((rows, PLANE * channels), jnp.bfloat16),
        in_specs=[SMEM] + [VMEM] * PLANE,
        out_specs=VMEM,
        scratch_shapes=[pltpu.VMEM((PLANE, channels, rows), jnp.float32)],
        name="assemble",
    )(where, *parts)


def plane_shards(tokens, norm_gain, in_weight, filter_taps, skip_gain):
    depth, block_cols = in_weight.shape
    chunk_cols = block_cols // STREAMS
    channels = skip_gain.shape[0] // PLANE
    group = skip_gain.shape[0] // filter_taps.shape[0]
    slab = lax.axis_index("fsdp")
    core = lax.axis_index("tp")
    plane, member = slab // PLANE, slab % PLANE
    y, x = member // SIDE, member % SIDE
    inner = jnp.where((plane == 1) | (plane == 2), 1, 0)
    lower = plane < 2
    where = jnp.stack([member, core]).astype(jnp.int32)

    turned = in_weight.T.reshape(STREAMS, chunk_cols, depth)
    stays = jnp.where(x == 0, turned[0], turned[2])
    along_y = jnp.where(x == 0, turned[2], turned[0])
    mine = [stays, moved(turned[1], to_x), moved(along_y, to_y)]
    offsets = [
        (3 * member + 2 * x) // PLANE,
        (3 * (member ^ 1) + 1) // PLANE,
        (3 * (member ^ 2) + 2 - 2 * x) // PLANE,
    ]

    slots = [[], [], [], []]
    for chunk in mine:
        paired = moved(chunk, to_pair)
        crossed = moved(chunk, to_middle)
        crossed_far = moved(paired, to_middle)
        end_near = moved(crossed, to_end)
        end_far = moved(crossed_far, to_end)
        slots[0].append([chunk])
        slots[1].append([paired])
        slots[2].append([crossed, end_near])
        slots[3].append([crossed_far, end_far])

    normed = normalized(tokens, norm_gain)
    mates = [normed, moved(normed, to_x), moved(normed, to_y), moved(normed, to_xy)]
    others = [moved(m, to_core) for m in mates]
    edge = moved(normed, lambda p, y, x, t: (p + 1, y, x, t) if (y, x, t) == (1, 1, 1) else None)
    edge = edge + moved(edge, lambda p, y, x, t: (p, 0, x, t) if (y, x, t) == (1, 1, 1) else None)
    edge = edge + moved(edge, lambda p, y, x, t: (p, y, 0, t) if (x, t) == (1, 1) else None)
    edge = edge + moved(edge, lambda p, y, x, t: (p, y, x, 0) if t == 1 else None)
    rows = jnp.concatenate([r for pair in zip(mates, others) for r in pair] + [edge], axis=0)

    proj = None
    places = [plane, plane ^ 1, jnp.where(lower, 2, 1), jnp.where(lower, 3, 0)]
    for place, chunks in zip(places, slots):
        table = jnp.stack([place, *offsets, inner]).astype(jnp.int32)
        proj = project(table, chunks, rows, proj)

    matrices = filter_matrices(where, filter_taps, chunk_cols // group)
    sections = channels // chunk_cols
    skip = lax.dynamic_index_in_dim(
        skip_gain.reshape(sections, PLANE, chunk_cols), member, 1, keepdims=False
    ).reshape(channels, 1)
    skip = jnp.broadcast_to(skip, (channels, filter_taps.shape[1]))
    own, for_x, for_y, for_xy = mixed_and_gated(where, proj, matrices, skip, chunk_cols)
    parts = [own, moved(for_x, to_x), moved(for_y, to_y), moved(for_xy, to_xy)]
    return assembled(where, parts, chunk_cols)


def fits_planes(tokens, in_weight, filter_taps, skip_gain, fsdp, tp):
    if fsdp != PLANE * PLANE or tp != 2:
        return False
    rows, cols = tokens.shape[0] // (fsdp * tp), in_weight.shape[1] // (fsdp * tp)
    channels, groups = skip_gain.shape[0], filter_taps.shape[0]
    return (
        cols % STREAMS == 0
        and cols // STREAMS * fsdp * tp == channels
        and (cols // STREAMS) % 64 == 0
        and (cols // STREAMS) % (channels // groups) == 0
        and (channels // groups) % 16 == 0
        and rows == filter_taps.shape[1]
        and rows == 128
        and in_weight.shape[0] % 256 == 0
    )


def solution(mesh):
    fsdp, tp = mesh.shape["fsdp"], mesh.shape["tp"]

    def run(tokens, norm_gain, in_weight, filter_taps, skip_gain):
        fits = fits_planes(tokens, in_weight, filter_taps, skip_gain, fsdp, tp)
        return jax.shard_map(
            plane_shards if fits else general_shards,
            mesh=mesh,
            in_specs=(P(AXES, None), P(), P(None, AXES), P("tp", None), P("tp")),
            out_specs=P("fsdp", "tp"),
            check_vma=False,
        )(tokens, norm_gain, in_weight, filter_taps, skip_gain)

    return run
```
